32 devices in a mesh: stn: 16 (over z, y, core), tm: 2 (over x).
Axes of the slice: x: 2, y: 2, z: 4, core: 2. Of those that a mesh axis runs over, the one named last changes fastest.
Arguments:
- voltages: int32 [512, 2, 32768], P('stn', None, 'tm'), may hold values from -127 to 127
- filter_taps: float32 [16, 1024], replicated, may hold values from -1.5 to 1.5
- reference_channel: int32 [1], replicated, may hold values from 0 to 511
- basis_inputs: int32 [8], replicated, may hold values from 0 to 511, as said below
Outputs:
- covariance: bfloat16 [512, 512, 1024], P(('stn', 'tm'))
- projection: float32 [512, 128], P(('stn', 'tm'))
- subspace_power: float32 [512, 32], P('stn', 'tm')
The draws below stay inside these ranges and needn't reach their ends.
Inputs may be any that keep to these rules, and one draw needn't show every extreme that they name: `basis_inputs`: 8 distinct input indices.
All inputs are finite; a program needn't handle non-finite values.
Results may differ from the reference program's by a relative error of at most 0.012.
Values may be sent and summed in bfloat16 or wider, within the bound.
No kernel may reach another device: no remote copies, remote signals or barrier semaphores. Data moves between devices by JAX's collectives and lax.ppermute only.
A program may use at most 192 MiB of HBM per device.

```python
import math
import jax
import jax.numpy as jnp
from jax import lax

INPUTS = 512
NFFT = 1024
FCH = 512
TAPS = 16
K = 8
T_DEV = 16
SPECTRA = 32
SAMPLES = 32768
N_TM = 2


def draw_voltages(key, part):
    level_key, noise_key, gain_key, tone_key = jax.random.split(key, 4)
    levels = jnp.array([12, 16, 24, 32, 48, 64, 80, 95], dtype=jnp.int32)
    level_index = jax.random.randint(level_key, (INPUTS,), 0, 8, dtype=jnp.int32)
    amplitude = levels[level_index][:, None, None]
    noise = jax.random.randint(noise_key, (INPUTS, 2, SAMPLES), -amplitude, amplitude + 1, dtype=jnp.int32)
    gain = jax.random.randint(gain_key, (INPUTS, 1, 1), -4, 5, dtype=jnp.int32)
    interferer = jax.random.randint(tone_key, (1, 2, SAMPLES), -8, 9, dtype=jnp.int32)
    return (noise + gain * interferer).astype(jnp.int32)


def draw_basis_inputs(key, part):
    order = jax.random.permutation(key, INPUTS)
    return order[:K].astype(jnp.int32)


def gaussian(own_key, dims, scale, reach, kind=jnp.bfloat16):
    drawn = scale * jax.random.normal(own_key, dims, jnp.float32)
    return jnp.clip(drawn, min=-reach, max=reach).astype(kind)


def setup_inputs(seed: int = 0) -> dict:
    streams_of = jax.random.split(jax.random.key(seed), 5)
    voltages = draw_voltages(jax.random.fold_in(streams_of[4], 71), 0)
    filter_taps = gaussian(streams_of[1], (TAPS, NFFT), TAPS ** -0.5, 1.5, jnp.float32)
    reference_channel = jax.random.randint(streams_of[2], (1,), 0, FCH).astype(jnp.int32)
    basis_inputs = draw_basis_inputs(jax.random.fold_in(streams_of[4], 71), 0)
    return {"voltages": voltages, "filter_taps": filter_taps, "reference_channel": reference_channel, "basis_inputs": basis_inputs}


def transform_tables():
    sample = jnp.arange(NFFT, dtype=jnp.int32)
    channel = jnp.arange(FCH, dtype=jnp.int32)
    phase = sample[:, None] * channel[None, :] % NFFT
    angle = phase.astype(jnp.float32) * (2.0 * math.pi / NFFT)
    factor = 1.0 / math.sqrt(NFFT)
    cosine = jnp.cos(angle) * factor
    sine = jnp.sin(angle) * factor
    table_re = jnp.stack([cosine, -sine], axis=2).reshape(NFFT, 2 * FCH).astype(jnp.bfloat16)
    table_im = jnp.stack([sine, cosine], axis=2).reshape(NFFT, 2 * FCH).astype(jnp.bfloat16)
    return (table_re, table_im)

def orthonormal(col_real, col_imag):
    basis_real = []
    basis_imag = []
    for column in range(col_real.shape[1]):
        vec_real = col_real[:, column]
        vec_imag = col_imag[:, column]
        for former in range(column):
            q_real = basis_real[former]
            q_imag = basis_imag[former]
            inner_real = jnp.sum(q_real * vec_real + q_imag * vec_imag)
            inner_imag = jnp.sum(q_real * vec_imag - q_imag * vec_real)
            vec_real = vec_real - (q_real * inner_real - q_imag * inner_imag)
            vec_imag = vec_imag - (q_real * inner_imag + q_imag * inner_real)
        inverse = lax.rsqrt(jnp.sum(vec_real * vec_real + vec_imag * vec_imag) + 1e-06)
        basis_real.append(vec_real * inverse)
        basis_imag.append(vec_imag * inverse)
    return (jnp.stack(basis_real, axis=1), jnp.stack(basis_imag, axis=1))

def reference(voltages, filter_taps, reference_channel, basis_inputs):
    table_re, table_im = transform_tables()

    def channelize(single):
        frames = (single.astype(jnp.float32) / 64.0).reshape(2, SPECTRA, NFFT)
        padded = jnp.pad(frames, ((0, 0), (TAPS - 1, 0), (0, 0)))
        accum = jnp.zeros((2, SPECTRA, NFFT), jnp.float32)
        for tap_index in range(TAPS):
            accum = accum + filter_taps[tap_index] * padded[:, tap_index:tap_index + SPECTRA, :]
        filtered = accum.astype(jnp.bfloat16)
        result = jnp.dot(filtered[0], table_re, preferred_element_type=jnp.float32)
        result = result + jnp.dot(filtered[1], table_im, preferred_element_type=jnp.float32)
        return result.astype(jnp.bfloat16)
    spectra = lax.map(channelize, voltages)

    def channel_data(index):
        piece = lax.dynamic_slice_in_dim(spectra, (2 * index).astype(jnp.int32), 2, 2)
        return (piece[:, :, 0].astype(jnp.float32), piece[:, :, 1].astype(jnp.float32))

    def averaged_cov(chan_real, chan_imag):
        block_real = chan_real.reshape(INPUTS, N_TM, T_DEV)
        block_imag = chan_imag.reshape(INPUTS, N_TM, T_DEV)
        sum_real = jnp.einsum('imt,jmt->mij', block_real, block_real) + jnp.einsum('imt,jmt->mij', block_imag, block_imag)
        sum_imag = jnp.einsum('imt,jmt->mij', block_imag, block_real) - jnp.einsum('imt,jmt->mij', block_real, block_imag)
        terms = jnp.concatenate([sum_real, sum_imag], axis=2)
        rounded = lax.optimization_barrier(terms.astype(jnp.bfloat16)).astype(jnp.float32)
        return lax.optimization_barrier(jnp.sum(rounded, axis=0)) / SPECTRA
    ref_real, ref_imag = channel_data(reference_channel[0])
    ref_cov = averaged_cov(ref_real, ref_imag)
    col_real = ref_cov[:, :INPUTS][:, basis_inputs]
    col_imag = ref_cov[:, INPUTS:][:, basis_inputs]
    basis_real, basis_imag = orthonormal(col_real, col_imag)
    low_real = lax.optimization_barrier(basis_real.astype(jnp.bfloat16)).astype(jnp.float32)
    low_imag = lax.optimization_barrier(basis_imag.astype(jnp.bfloat16)).astype(jnp.float32)
    highest = lax.Precision.HIGHEST

    def per_channel(index):
        chan_real, chan_imag = channel_data(index)
        averaged = averaged_cov(chan_real, chan_imag)
        cov_real = averaged[:, :INPUTS]
        cov_imag = averaged[:, INPUTS:]
        prod_real = jnp.dot(cov_real, basis_real, precision=highest) - jnp.dot(cov_imag, basis_imag, precision=highest)
        prod_imag = jnp.dot(cov_real, basis_imag, precision=highest) + jnp.dot(cov_imag, basis_real, precision=highest)
        proj_real = jnp.dot(basis_real.T, prod_real, precision=highest) + jnp.dot(basis_imag.T, prod_imag, precision=highest)
        proj_imag = jnp.dot(basis_real.T, prod_imag, precision=highest) - jnp.dot(basis_imag.T, prod_real, precision=highest)
        projection = jnp.concatenate([proj_real.reshape(-1), proj_imag.reshape(-1)])
        sub_real = jnp.dot(low_real.T, chan_real, precision=highest) + jnp.dot(low_imag.T, chan_imag, precision=highest)
        sub_imag = jnp.dot(low_real.T, chan_imag, precision=highest) - jnp.dot(low_imag.T, chan_real, precision=highest)
        power = lax.optimization_barrier(jnp.sum(sub_real * sub_real + sub_imag * sub_imag, axis=0))
        return (averaged.astype(jnp.bfloat16), projection, power)
    covariance, projection, power = lax.map(per_channel, jnp.arange(FCH, dtype=jnp.int32))
    return (covariance, projection, power)
```

```python
import functools
import math

import jax
import jax.numpy as jnp
from jax import lax
from jax.experimental import pallas as pl
from jax.experimental.pallas import tpu as pltpu
from jax.sharding import PartitionSpec as P

NFFT = 1024
FCH = 512


def passed_along(block, axis, distance):
    devices = range(lax.axis_size(axis))
    route = [(i - distance, i) for i in devices if i - distance in devices]
    return lax.ppermute(block, axis, route)


def spread(shard, axis, root):
    mine = lax.axis_index(axis) == root
    return lax.psum(jnp.where(mine, shard, jnp.zeros_like(shard)), axis)


def transform_tables():
    sample = jnp.arange(NFFT, dtype=jnp.int32)
    channel = jnp.arange(FCH, dtype=jnp.int32)
    phase = sample[:, None] * channel[None, :] % NFFT
    angle = phase.astype(jnp.float32) * (2.0 * math.pi / NFFT)
    factor = 1.0 / math.sqrt(NFFT)
    cosine = jnp.cos(angle) * factor
    sine = jnp.sin(angle) * factor
    table_re = jnp.stack([cosine, -sine], axis=2).reshape(NFFT, 2 * FCH).astype(jnp.bfloat16)
    table_im = jnp.stack([sine, cosine], axis=2).reshape(NFFT, 2 * FCH).astype(jnp.bfloat16)
    return (table_re, table_im)


def orthonormal(col_real, col_imag):
    basis_real = []
    basis_imag = []
    for column in range(col_real.shape[1]):
        vec_real = col_real[:, column]
        vec_imag = col_imag[:, column]
        for former in range(column):
            q_real = basis_real[former]
            q_imag = basis_imag[former]
            inner_real = jnp.sum(q_real * vec_real + q_imag * vec_imag)
            inner_imag = jnp.sum(q_real * vec_imag - q_imag * vec_real)
            vec_real = vec_real - (q_real * inner_real - q_imag * inner_imag)
            vec_imag = vec_imag - (q_real * inner_imag + q_imag * inner_real)
        inverse = lax.rsqrt(jnp.sum(vec_real * vec_real + vec_imag * vec_imag) + 1e-06)
        basis_real.append(vec_real * inverse)
        basis_imag.append(vec_imag * inverse)
    return (jnp.stack(basis_real, axis=1), jnp.stack(basis_imag, axis=1))


def block_sums(part_real, part_imag):
    sum_real = jnp.einsum("itc,jtc->cij", part_real, part_real, preferred_element_type=jnp.float32)
    sum_real = sum_real + jnp.einsum(
        "itc,jtc->cij", part_imag, part_imag, preferred_element_type=jnp.float32
    )
    sum_imag = jnp.einsum("itc,jtc->cij", part_imag, part_real, preferred_element_type=jnp.float32)
    sum_imag = sum_imag - jnp.einsum(
        "itc,jtc->cij", part_real, part_imag, preferred_element_type=jnp.float32
    )
    return (sum_real, sum_imag)


def blockwise_covariance(full_real, full_imag, blocks, frames):
    inputs_all = full_real.shape[0]
    chans = full_real.shape[2]

    def add_block(index, total):
        first = index * frames
        part_real = lax.dynamic_slice_in_dim(full_real, first, frames, 1)
        part_imag = lax.dynamic_slice_in_dim(full_imag, first, frames, 1)
        sum_real, sum_imag = block_sums(part_real, part_imag)
        terms = jnp.concatenate([sum_real, sum_imag], axis=2)
        rounded = lax.optimization_barrier(terms.astype(jnp.bfloat16)).astype(jnp.float32)
        return total + rounded

    start = jnp.zeros((chans, inputs_all, 2 * inputs_all), jnp.float32)
    return lax.fori_loop(0, blocks, add_block, start)


def plain_plan(voltages, filter_taps, reference_channel, basis_inputs):
    blocks = lax.axis_size("tm")
    local_inputs = voltages.shape[0]
    inputs_all = local_inputs * lax.axis_size("stn")
    frames = voltages.shape[2] // NFFT
    spectra_total = frames * blocks
    tap_count = filter_taps.shape[0]
    signal = (
        (voltages.astype(jnp.float32) / 64.0)
        .astype(jnp.bfloat16)
        .reshape(local_inputs, 2, frames, NFFT)
    )
    earlier = passed_along(signal[:, :, frames - (tap_count - 1) :, :], "tm", 1)
    extended = jnp.concatenate([earlier, signal], axis=2)
    accum = jnp.zeros((local_inputs, 2, frames, NFFT), jnp.float32)
    for tap_index in range(tap_count):
        accum = accum + filter_taps[tap_index] * extended[
            :, :, tap_index : tap_index + frames, :
        ].astype(jnp.float32)
    filtered = accum.astype(jnp.bfloat16)
    table_re, table_im = transform_tables()
    spectra = jnp.einsum(
        "itn,nc->itc", filtered[:, 0], table_re, preferred_element_type=jnp.float32
    )
    spectra = spectra + jnp.einsum(
        "itn,nc->itc", filtered[:, 1], table_im, preferred_element_type=jnp.float32
    )
    spectra = spectra.astype(jnp.bfloat16)
    rows_iota = jnp.arange(inputs_all, dtype=jnp.int32)[:, None]
    moved = lax.all_to_all(
        lax.all_to_all(spectra, "stn", split_axis=2, concat_axis=0, tiled=True),
        "tm",
        split_axis=2,
        concat_axis=1,
        tiled=True,
    )
    chan_owned = moved.shape[2] // 2
    joined = moved.reshape(inputs_all, spectra_total, chan_owned, 2)
    full_real = joined[:, :, :, 0]
    full_imag = joined[:, :, :, 1]
    summed = blockwise_covariance(full_real, full_imag, blocks, frames)
    averaged = summed / spectra_total
    covariance = averaged.astype(jnp.bfloat16)
    highest = lax.Precision.HIGHEST
    selector = rows_iota == basis_inputs[None, :]
    ref_index = reference_channel[0]
    root_index = ref_index // chan_owned
    local_index = ref_index % chan_owned
    ref_rows = lax.dynamic_slice_in_dim(averaged, local_index, 1, 0)[0]
    onehot = selector.astype(jnp.float32)
    picked = jnp.stack(
        [
            jnp.dot(ref_rows[:, :inputs_all], onehot, precision=highest),
            jnp.dot(ref_rows[:, inputs_all:], onehot, precision=highest),
        ]
    )
    picked = spread(picked.astype(jnp.bfloat16), ("stn", "tm"), root_index).astype(picked.dtype)
    col_real = picked[0]
    col_imag = picked[1]
    basis_real, basis_imag = orthonormal(col_real, col_imag)
    cov_real = averaged[:, :, :inputs_all]
    cov_imag = averaged[:, :, inputs_all:]
    prod_real = jnp.einsum("cij,jk->cik", cov_real, basis_real, precision=highest)
    prod_real = prod_real - jnp.einsum("cij,jk->cik", cov_imag, basis_imag, precision=highest)
    prod_imag = jnp.einsum("cij,jk->cik", cov_real, basis_imag, precision=highest)
    prod_imag = prod_imag + jnp.einsum("cij,jk->cik", cov_imag, basis_real, precision=highest)
    proj_real = jnp.einsum("ik,cil->ckl", basis_real, prod_real, precision=highest)
    proj_real = proj_real + jnp.einsum("ik,cil->ckl", basis_imag, prod_imag, precision=highest)
    proj_imag = jnp.einsum("ik,cil->ckl", basis_real, prod_imag, precision=highest)
    proj_imag = proj_imag - jnp.einsum("ik,cil->ckl", basis_imag, prod_real, precision=highest)
    projection = jnp.concatenate(
        [proj_real.reshape(chan_owned, -1), proj_imag.reshape(chan_owned, -1)], axis=1
    )
    low_real = basis_real.astype(jnp.bfloat16)
    low_imag = basis_imag.astype(jnp.bfloat16)
    sub_real = jnp.einsum("ik,itc->kct", low_real, full_real, preferred_element_type=jnp.float32)
    sub_real = sub_real + jnp.einsum(
        "ik,itc->kct", low_imag, full_imag, preferred_element_type=jnp.float32
    )
    sub_imag = jnp.einsum("ik,itc->kct", low_real, full_imag, preferred_element_type=jnp.float32)
    sub_imag = sub_imag - jnp.einsum(
        "ik,itc->kct", low_imag, full_real, preferred_element_type=jnp.float32
    )
    owned_power = jnp.sum(sub_real * sub_real + sub_imag * sub_imag, axis=0)
    subspace_power = lax.all_to_all(owned_power, "tm", split_axis=1, concat_axis=0, tiled=True)
    return (covariance, projection, subspace_power)


LANES = 128
SUB = 8
ROWS = 16
NT_DIMS = (((1,), (1,)), ((), ()))


def nt_dot(a, b, precision=None):
    return lax.dot_general(a, b, NT_DIMS, precision=precision, preferred_element_type=jnp.float32)


class Plan:
    def __init__(self, voltages, filter_taps):
        self.blocks = lax.axis_size("tm")
        self.devices = lax.axis_size("stn") * self.blocks
        self.taps, self.nfft = filter_taps.shape
        self.chans = self.nfft // 2 // self.devices
        self.inputs = voltages.shape[0] // self.blocks
        self.inputs_all = voltages.shape[0] * lax.axis_size("stn")
        self.frames = voltages.shape[2] // self.nfft
        self.spectra = self.frames * self.blocks
        self.tiles = 2 * self.nfft // LANES
        self.group = LANES // self.spectra
        self.quads = self.chans // max(self.group, 1)
        self.chunk = 2 * self.quads * self.inputs
        self.extra = self.inputs // 2

    def packed(self):
        return (
            self.blocks == 2
            and self.group == 4
            and self.group * self.spectra == LANES
            and 2 * self.quads == SUB
            and self.inputs == ROWS
            and self.tiles == ROWS
        )


def table_kernel(plan, rows, out_ref):
    shape = (rows, LANES)
    row = lax.broadcasted_iota(jnp.int32, shape, 0) + pl.program_id(0) * rows
    lane = lax.broadcasted_iota(jnp.int32, shape, 1)
    per_dest = plan.group * 2 * plan.quads
    dest = lax.div(row, per_dest)
    member = lax.rem(lax.div(row, 2 * plan.quads), plan.group)
    part = lax.rem(lax.div(row, plan.quads), 2)
    quad = lax.rem(row, plan.quads)
    channel = dest * plan.chans + quad * plan.group + member
    unit = 2.0 * math.pi / plan.nfft
    phase = lax.rem(lane * channel + part * (plan.nfft // 4), plan.nfft)
    angle = phase.astype(jnp.float32) * unit
    factor = 1.0 / math.sqrt(plan.nfft)
    cosine = jnp.cos(angle) * factor
    sine = jnp.sin(angle) * factor
    turn = lax.rem(channel * LANES, plan.nfft).astype(jnp.float32) * unit
    turn_cos = jnp.cos(turn)
    turn_sin = jnp.sin(turn)
    for tile in range(plan.nfft // LANES):
        first = 2 * tile * LANES
        out_ref[:, first : first + LANES] = cosine.astype(jnp.bfloat16)
        out_ref[:, first + LANES : first + 2 * LANES] = sine.astype(jnp.bfloat16)
        cosine, sine = (
            cosine * turn_cos - sine * turn_sin,
            sine * turn_cos + cosine * turn_sin,
        )


def transform_table(plan):
    rows = 128
    total = plan.nfft
    return pl.pallas_call(
        functools.partial(table_kernel, plan, rows),
        grid=(total // rows,),
        out_specs=pl.BlockSpec((rows, 2 * plan.nfft), lambda r: (r, 0)),
        out_shape=jax.ShapeDtypeStruct((total, 2 * plan.nfft), jnp.bfloat16),
        name="table",
    )()


def lane_iota(rows):
    return lax.broadcasted_iota(jnp.int32, (rows, LANES), 1)


def regroup(values):
    lane = lane_iota(SUB)
    low = lane < 64
    even = (lane & 32) == 0
    v0, v1, v2, v3 = values
    x0 = jnp.where(low, v0, pltpu.roll(v2, 64, 1))
    y0 = jnp.where(low, pltpu.roll(v0, 64, 1), v2)
    x1 = jnp.where(low, v1, pltpu.roll(v3, 64, 1))
    y1 = jnp.where(low, pltpu.roll(v1, 64, 1), v3)
    out = []
    for a, b in ((x0, x1), (y0, y1)):
        out.append(jnp.where(even, a, pltpu.roll(b, 32, 1)))
        out.append(jnp.where(even, pltpu.roll(a, 96, 1), b))
    return out


def channelize_kernel(
    plan, half, where_ref, own_ref, recv_ref, taps_ref, table_hbm, out_ref, table, sig, filt, low, prod, spread_f32, sem
):
    step = pl.program_id(0)
    block = where_ref[0]
    copy = pltpu.make_async_copy(table_hbm, table, sem)

    @pl.when(step == 0)
    def _():
        copy.start()

    frames, spectra, taps = plan.frames, plan.spectra, plan.taps
    span = frames * ROWS

    def one_input(i, carry):
        own_at = pl.multiple_of(block * span, span)
        recv_at = pl.multiple_of((1 - block) * span, span)
        start = pl.multiple_of(i * span, span)
        sig[pl.ds(own_at, span), :] = own_ref[pl.ds(start, span), :].astype(jnp.float32)
        sig[pl.ds(recv_at, span), :] = recv_ref[pl.ds(start, span), :].astype(jnp.float32)
        base = pl.multiple_of(i * (spectra * ROWS), spectra * ROWS)
        for sub in range(ROWS // SUB):
            tap = [taps_ref[k * ROWS + sub * SUB : k * ROWS + (sub + 1) * SUB, :] for k in range(taps)]
            data = [sig[f * ROWS + sub * SUB : f * ROWS + (sub + 1) * SUB, :] for f in range(spectra)]
            for t in range(spectra):
                acc = None
                for k in range(max(0, taps - 1 - t), taps):
                    term = tap[k] * data[t - (taps - 1) + k]
                    acc = term if acc is None else acc + term
                filt[pl.ds(base + t * ROWS + sub * SUB, SUB), :] = acc
        return carry

    lax.fori_loop(0, half, one_input, 0)
    for tile in range(plan.tiles):
        picked = filt[pl.ds(tile, half * spectra, stride=ROWS), :]
        low[:, tile * LANES : (tile + 1) * LANES] = picked.astype(jnp.bfloat16)

    @pl.when(step == 0)
    def _():
        copy.wait()

    prod[...] = nt_dot(table[...], low[...])
    per_dest = plan.group * SUB

    def one_dest(d, carry):
        rows = pl.multiple_of(d * per_dest, per_dest)
        for part in range(half // plan.group):
            cols = slice(part * LANES, (part + 1) * LANES)
            moved = regroup([prod[pl.ds(rows + c * SUB, SUB), cols] for c in range(plan.group)])
            for b in range(plan.group):
                at = d * (SUB * ROWS) + step * half + part * plan.group + b
                spread_f32[pl.ds(at, SUB, stride=ROWS), :] = moved[b]
        return carry

    lax.fori_loop(0, plan.devices, one_dest, 0)

    @pl.when(step == pl.num_programs(0) - 1)
    def _():
        channel = where_ref[1]
        owner = lax.div(channel, plan.chans)
        local = lax.rem(channel, plan.chans)
        quad = lax.div(local, plan.group)
        member = lax.rem(local, plan.group)
        lane = lane_iota(ROWS)
        tiles = []
        for part in range(2):
            at = pl.multiple_of((owner * SUB + part * plan.quads + quad) * ROWS, ROWS)
            tiles.append(spread_f32[pl.ds(at, ROWS), :])
        shift = LANES - member * plan.spectra
        real = pltpu.roll(tiles[0], lax.rem(shift, LANES), 1)
        imag = pltpu.roll(tiles[1], lax.rem(shift + plan.spectra, LANES), 1)
        both = jnp.where(lane < plan.spectra, real, imag)
        folded = jnp.where(lane_iota(SUB) < 64, both[:SUB], pltpu.roll(both[SUB:], 64, 1))
        folded = folded.astype(jnp.bfloat16)

        def finish(d, carry):
            at = pl.multiple_of(d * plan.chunk, plan.chunk)
            out_ref[d, : plan.chunk, :] = spread_f32[pl.ds(at, plan.chunk), :].astype(jnp.bfloat16)
            out_ref[d, plan.chunk :, :] = folded
            return carry

        lax.fori_loop(0, plan.devices, finish, 0)


def channelize(plan, where, own, recv, taps, table):
    half = plan.inputs // 2
    rows = half * plan.frames * ROWS
    out = (plan.devices, plan.chunk + plan.extra, LANES)
    return pl.pallas_call(
        functools.partial(channelize_kernel, plan, half),
        grid_spec=pltpu.PrefetchScalarGridSpec(
            num_scalar_prefetch=1,
            grid=(2,),
            in_specs=[
                pl.BlockSpec((rows, LANES), lambda g, w: (w[0] * 2 + g, 0)),
                pl.BlockSpec((rows, LANES), lambda g, w: (g, 0)),
                pl.BlockSpec(taps.shape, lambda g, w: (0, 0)),
                pl.BlockSpec(memory_space=pl.ANY),
            ],
            out_specs=pl.BlockSpec(out, lambda g, w: (0, 0, 0)),
            scratch_shapes=[
                pltpu.VMEM(table.shape, jnp.bfloat16),
                pltpu.VMEM((plan.spectra * ROWS, LANES), jnp.float32),
                pltpu.VMEM((half * plan.spectra * ROWS, LANES), jnp.float32),
                pltpu.VMEM((half * plan.spectra, 2 * plan.nfft), jnp.bfloat16),
                pltpu.VMEM((plan.nfft, half * plan.spectra), jnp.float32),
                pltpu.VMEM((plan.devices * plan.chunk, LANES), jnp.float32),
                pltpu.SemaphoreType.DMA(()),
            ],
        ),
        out_shape=jax.ShapeDtypeStruct(out, jnp.bfloat16),
        name="channelize",
    )(where, own, recv, taps, table)


def pair_of(recv_ref, plan, quad):
    shape = (plan.inputs_all, LANES)
    real = recv_ref[:, quad * ROWS : (quad + 1) * ROWS, :].reshape(shape)
    at = (plan.quads + quad) * ROWS
    imag = recv_ref[:, at : at + ROWS, :].reshape(shape)
    return real, imag


def inverse_root(value):
    y = lax.rsqrt(value)
    return y * (1.5 - 0.5 * value * y * y)


def basis_kernel(plan, count, recv_ref, picks_ref, proj_ref, power_ref):
    highest = lax.Precision.HIGHEST
    span = plan.spectra
    folded = recv_ref[:, plan.chunk :, :].astype(jnp.float32)
    turned = pltpu.roll(folded.reshape(-1, LANES), 64, 1).reshape(folded.shape)
    ref = jnp.concatenate([folded, turned], axis=1).reshape(plan.inputs_all, LANES)
    ref = ref.astype(jnp.bfloat16)
    rows = lax.broadcasted_iota(jnp.int32, (count, plan.inputs_all), 1)
    onehot = (rows == picks_ref[...]).astype(jnp.float32).astype(jnp.bfloat16)
    chosen = jnp.dot(onehot, ref, preferred_element_type=jnp.float32)
    lane = lane_iota(count)
    zero = jnp.zeros_like(chosen)
    left = jnp.where(lane < 2 * span, chosen, zero)
    cross = jnp.where(
        lane < span,
        -pltpu.roll(chosen, LANES - span, 1),
        jnp.where(lane < 2 * span, pltpu.roll(chosen, span, 1), zero),
    )
    real = nt_dot(left.astype(jnp.bfloat16), ref) / span
    imag = nt_dot(cross.astype(jnp.bfloat16), ref) / span
    index = lax.broadcasted_iota(jnp.int32, real.shape, 0)
    for j in range(count):
        vr = jnp.broadcast_to(real[j : j + 1], real.shape)
        vi = jnp.broadcast_to(imag[j : j + 1], real.shape)
        inner_r = jnp.sum(vr * real + vi * imag, axis=1, keepdims=True)
        inner_i = jnp.sum(vr * imag - vi * real, axis=1, keepdims=True)
        inverse = inverse_root(inner_r[j : j + 1] + 1e-06)
        qr = vr * inverse
        qi = vi * inverse
        inner_r = inner_r * inverse
        inner_i = inner_i * inverse
        later = index > j
        this = index == j
        next_r = real - (qr * inner_r - qi * inner_i)
        next_i = imag - (qr * inner_i + qi * inner_r)
        real = jnp.where(this, qr, jnp.where(later, next_r, real))
        imag = jnp.where(this, qi, jnp.where(later, next_i, imag))
    levels = []
    rest_r, rest_i = real, imag
    for _ in range(3):
        top_r = rest_r.astype(jnp.bfloat16).astype(jnp.float32)
        top_i = rest_i.astype(jnp.bfloat16).astype(jnp.float32)
        levels += [top_r, top_i]
        rest_r = rest_r - top_r
        rest_i = rest_i - top_i
    stack = jnp.concatenate(levels, axis=0).astype(jnp.bfloat16)
    members = plan.group * count
    row = lax.broadcasted_iota(jnp.int32, (members, LANES), 0)
    col = lax.broadcasted_iota(jnp.int32, (members, LANES), 1)
    mine = lax.div(row, count) == lax.div(col, span)
    size = count * count
    lead = lax.broadcasted_iota(jnp.int32, (count, 2 * size), 0)
    spot = lax.broadcasted_iota(jnp.int32, (count, 2 * size), 1)
    fits = lax.rem(spot, count) == lead
    put_r = jnp.where(fits & (spot < size), 1.0, 0.0)
    put_i = jnp.where(fits & (spot >= size), 1.0, 0.0)
    wide = lax.broadcasted_iota(jnp.int32, (members, 2 * size), 1)
    tall = lax.broadcasted_iota(jnp.int32, (members, 2 * size), 0)
    keep = lax.rem(lax.div(wide, count), count) == lax.rem(tall, count)
    for quad in range(plan.quads):
        xr, xi = pair_of(recv_ref, plan, quad)
        sr = jnp.dot(stack, xr, preferred_element_type=jnp.float32)
        si = jnp.dot(stack, xi, preferred_element_type=jnp.float32)
        piece = lambda s, n: s[n * count : (n + 1) * count]
        low_r = piece(sr, 0) + piece(si, 1)
        low_i = piece(si, 0) - piece(sr, 1)
        power_ref[quad : quad + 1, :] = jnp.sum(low_r * low_r + low_i * low_i, axis=0, keepdims=True)
        yr = low_r + ((piece(sr, 2) + piece(si, 3)) + (piece(sr, 4) + piece(si, 5)))
        yi = low_i + ((piece(si, 2) - piece(sr, 3)) + (piece(si, 4) - piece(sr, 5)))
        tiled_r = jnp.where(mine, jnp.concatenate([yr] * plan.group, axis=0), 0.0)
        tiled_i = jnp.where(mine, jnp.concatenate([yi] * plan.group, axis=0), 0.0)
        both = jnp.concatenate([yr, yi], axis=1)
        left_r = jnp.concatenate([tiled_r, tiled_i], axis=1)
        left_i = jnp.concatenate([tiled_i, -tiled_r], axis=1)
        gram_r = nt_dot(left_r, both, highest) / span
        gram_i = nt_dot(left_i, both, highest) / span
        placed = jnp.dot(gram_r, put_r, precision=highest) + jnp.dot(gram_i, put_i, precision=highest)
        placed = jnp.where(keep, placed, 0.0).reshape(plan.group, count, 2 * size)
        proj_ref[quad * plan.group : (quad + 1) * plan.group, :] = jnp.sum(placed, axis=1)


def subspace(plan, recv, basis_inputs):
    count = basis_inputs.shape[0]
    return pl.pallas_call(
        functools.partial(basis_kernel, plan, count),
        out_shape=(
            jax.ShapeDtypeStruct((plan.chans, 2 * count * count), jnp.float32),
            jax.ShapeDtypeStruct((plan.quads, LANES), jnp.float32),
        ),
        name="subspace",
    )(recv, basis_inputs.reshape(count, 1))


def covariance_kernel(plan, real_ref, imag_ref, out_ref):
    member = lax.rem(pl.program_id(0), plan.group)
    shape = (plan.inputs_all, LANES)
    real = real_ref[...].reshape(shape)
    imag = imag_ref[...].reshape(shape)
    inside = lax.div(lax.broadcasted_iota(jnp.int32, (1, LANES), 1), plan.spectra) == member
    mask = jnp.where(inside, 1.0 / plan.spectra, 0.0).astype(jnp.bfloat16)
    left_r = real * mask
    left_i = imag * mask
    right = jnp.concatenate([real, imag], axis=1)
    total = plan.inputs_all
    out_ref[0, :, :total] = nt_dot(jnp.concatenate([left_r, left_i], axis=1), right).astype(jnp.bfloat16)
    out_ref[0, :, total:] = nt_dot(jnp.concatenate([left_i, -left_r], axis=1), right).astype(jnp.bfloat16)


def covariances(plan, recv):
    out = (plan.chans, plan.inputs_all, 2 * plan.inputs_all)
    block = (plan.devices, ROWS, LANES)
    return pl.pallas_call(
        functools.partial(covariance_kernel, plan),
        grid=(plan.chans,),
        in_specs=[
            pl.BlockSpec(block, lambda c: (0, c // plan.group, 0)),
            pl.BlockSpec(block, lambda c: (0, plan.quads + c // plan.group, 0)),
        ],
        out_specs=pl.BlockSpec((1, *out[1:]), lambda c: (c, 0, 0)),
        out_shape=jax.ShapeDtypeStruct(out, jnp.bfloat16),
        name="covariance",
    )(recv, recv)


def packed_plan(plan, voltages, filter_taps, reference_channel, basis_inputs):
    block = lax.axis_index("tm")
    kept = plan.inputs * plan.frames * plan.tiles
    view = voltages.reshape(voltages.shape[0], 2, -1, LANES).transpose(0, 2, 1, 3).reshape(-1, LANES)
    sent = lax.dynamic_slice_in_dim(view, (1 - block) * kept, kept, 0).astype(jnp.bfloat16)
    recv = lax.ppermute(sent, "tm", [(0, 1), (1, 0)])
    taps = (filter_taps / 64.0).reshape(plan.taps, -1, 1, LANES)
    taps = jnp.broadcast_to(taps, (plan.taps, plan.tiles // 2, 2, LANES)).reshape(-1, LANES)
    table = transform_table(plan)
    where = jnp.stack([block.astype(jnp.int32), reference_channel[0]])
    spectra = channelize(plan, where, view, recv, taps, table)
    moved = lax.all_to_all(spectra, ("stn", "tm"), split_axis=0, concat_axis=0, tiled=True)
    projection, power = subspace(plan, moved, basis_inputs)
    power = power.reshape(plan.chans, plan.spectra)
    subspace_power = lax.all_to_all(power, "tm", split_axis=1, concat_axis=0, tiled=True)
    covariance = covariances(plan, moved)
    return (covariance, projection, subspace_power)


def on_device(voltages, filter_taps, reference_channel, basis_inputs):
    plan = Plan(voltages, filter_taps)
    body = functools.partial(packed_plan, plan) if plan.packed() else plain_plan
    return body(voltages, filter_taps, reference_channel, basis_inputs)


def solution(mesh):
    return jax.shard_map(
        on_device,
        mesh=mesh,
        in_specs=(P("stn", None, "tm"), P(), P(), P()),
        out_specs=(P(("stn", "tm"), None, None), P(("stn", "tm"), None), P("stn", "tm")),
        check_vma=False,
    )
```

```python
import functools
import math

import jax
import jax.numpy as jnp
from jax import lax
from jax.experimental import pallas as pl
from jax.experimental.pallas import tpu as pltpu
from jax.sharding import PartitionSpec as P

NFFT = 1024
FCH = 512


def passed_along(block, axis, distance):
    devices = range(lax.axis_size(axis))
    route = [(i - distance, i) for i in devices if i - distance in devices]
    return lax.ppermute(block, axis, route)


def spread(shard, axis, root):
    mine = lax.axis_index(axis) == root
    return lax.psum(jnp.where(mine, shard, jnp.zeros_like(shard)), axis)


def transform_tables():
    sample = jnp.arange(NFFT, dtype=jnp.int32)
    channel = jnp.arange(FCH, dtype=jnp.int32)
    phase = sample[:, None] * channel[None, :] % NFFT
    angle = phase.astype(jnp.float32) * (2.0 * math.pi / NFFT)
    factor = 1.0 / math.sqrt(NFFT)
    cosine = jnp.cos(angle) * factor
    sine = jnp.sin(angle) * factor
    table_re = jnp.stack([cosine, -sine], axis=2).reshape(NFFT, 2 * FCH).astype(jnp.bfloat16)
    table_im = jnp.stack([sine, cosine], axis=2).reshape(NFFT, 2 * FCH).astype(jnp.bfloat16)
    return (table_re, table_im)


def orthonormal(col_real, col_imag):
    basis_real = []
    basis_imag = []
    for column in range(col_real.shape[1]):
        vec_real = col_real[:, column]
        vec_imag = col_imag[:, column]
        for former in range(column):
            q_real = basis_real[former]
            q_imag = basis_imag[former]
            inner_real = jnp.sum(q_real * vec_real + q_imag * vec_imag)
            inner_imag = jnp.sum(q_real * vec_imag - q_imag * vec_real)
            vec_real = vec_real - (q_real * inner_real - q_imag * inner_imag)
            vec_imag = vec_imag - (q_real * inner_imag + q_imag * inner_real)
        inverse = lax.rsqrt(jnp.sum(vec_real * vec_real + vec_imag * vec_imag) + 1e-06)
        basis_real.append(vec_real * inverse)
        basis_imag.append(vec_imag * inverse)
    return (jnp.stack(basis_real, axis=1), jnp.stack(basis_imag, axis=1))


def block_sums(part_real, part_imag):
    sum_real = jnp.einsum("itc,jtc->cij", part_real, part_real, preferred_element_type=jnp.float32)
    sum_real = sum_real + jnp.einsum(
        "itc,jtc->cij", part_imag, part_imag, preferred_element_type=jnp.float32
    )
    sum_imag = jnp.einsum("itc,jtc->cij", part_imag, part_real, preferred_element_type=jnp.float32)
    sum_imag = sum_imag - jnp.einsum(
        "itc,jtc->cij", part_real, part_imag, preferred_element_type=jnp.float32
    )
    return (sum_real, sum_imag)


def blockwise_covariance(full_real, full_imag, blocks, frames):
    inputs_all = full_real.shape[0]
    chans = full_real.shape[2]

    def add_block(index, total):
        first = index * frames
        part_real = lax.dynamic_slice_in_dim(full_real, first, frames, 1)
        part_imag = lax.dynamic_slice_in_dim(full_imag, first, frames, 1)
        sum_real, sum_imag = block_sums(part_real, part_imag)
        terms = jnp.concatenate([sum_real, sum_imag], axis=2)
        rounded = lax.optimization_barrier(terms.astype(jnp.bfloat16)).astype(jnp.float32)
        return total + rounded

    start = jnp.zeros((chans, inputs_all, 2 * inputs_all), jnp.float32)
    return lax.fori_loop(0, blocks, add_block, start)


def plain_plan(voltages, filter_taps, reference_channel, basis_inputs):
    blocks = lax.axis_size("tm")
    local_inputs = voltages.shape[0]
    inputs_all = local_inputs * lax.axis_size("stn")
    frames = voltages.shape[2] // NFFT
    spectra_total = frames * blocks
    tap_count = filter_taps.shape[0]
    signal = (
        (voltages.astype(jnp.float32) / 64.0)
        .astype(jnp.bfloat16)
        .reshape(local_inputs, 2, frames, NFFT)
    )
    earlier = passed_along(signal[:, :, frames - (tap_count - 1) :, :], "tm", 1)
    extended = jnp.concatenate([earlier, signal], axis=2)
    accum = jnp.zeros((local_inputs, 2, frames, NFFT), jnp.float32)
    for tap_index in range(tap_count):
        accum = accum + filter_taps[tap_index] * extended[
            :, :, tap_index : tap_index + frames, :
        ].astype(jnp.float32)
    filtered = accum.astype(jnp.bfloat16)
    table_re, table_im = transform_tables()
    spectra = jnp.einsum(
        "itn,nc->itc", filtered[:, 0], table_re, preferred_element_type=jnp.float32
    )
    spectra = spectra + jnp.einsum(
        "itn,nc->itc", filtered[:, 1], table_im, preferred_element_type=jnp.float32
    )
    spectra = spectra.astype(jnp.bfloat16)
    rows_iota = jnp.arange(inputs_all, dtype=jnp.int32)[:, None]
    moved = lax.all_to_all(
        lax.all_to_all(spectra, "stn", split_axis=2, concat_axis=0, tiled=True),
        "tm",
        split_axis=2,
        concat_axis=1,
        tiled=True,
    )
    chan_owned = moved.shape[2] // 2
    joined = moved.reshape(inputs_all, spectra_total, chan_owned, 2)
    full_real = joined[:, :, :, 0]
    full_imag = joined[:, :, :, 1]
    summed = blockwise_covariance(full_real, full_imag, blocks, frames)
    averaged = summed / spectra_total
    covariance = averaged.astype(jnp.bfloat16)
    highest = lax.Precision.HIGHEST
    selector = rows_iota == basis_inputs[None, :]
    ref_index = reference_channel[0]
    root_index = ref_index // chan_owned
    local_index = ref_index % chan_owned
    ref_rows = lax.dynamic_slice_in_dim(averaged, local_index, 1, 0)[0]
    onehot = selector.astype(jnp.float32)
    picked = jnp.stack(
        [
            jnp.dot(ref_rows[:, :inputs_all], onehot, precision=highest),
            jnp.dot(ref_rows[:, inputs_all:], onehot, precision=highest),
        ]
    )
    picked = spread(picked.astype(jnp.bfloat16), ("stn", "tm"), root_index).astype(picked.dtype)
    col_real = picked[0]
    col_imag = picked[1]
    basis_real, basis_imag = orthonormal(col_real, col_imag)
    cov_real = averaged[:, :, :inputs_all]
    cov_imag = averaged[:, :, inputs_all:]
    prod_real = jnp.einsum("cij,jk->cik", cov_real, basis_real, precision=highest)
    prod_real = prod_real - jnp.einsum("cij,jk->cik", cov_imag, basis_imag, precision=highest)
    prod_imag = jnp.einsum("cij,jk->cik", cov_real, basis_imag, precision=highest)
    prod_imag = prod_imag + jnp.einsum("cij,jk->cik", cov_imag, basis_real, precision=highest)
    proj_real = jnp.einsum("ik,cil->ckl", basis_real, prod_real, precision=highest)
    proj_real = proj_real + jnp.einsum("ik,cil->ckl", basis_imag, prod_imag, precision=highest)
    proj_imag = jnp.einsum("ik,cil->ckl", basis_real, prod_imag, precision=highest)
    proj_imag = proj_imag - jnp.einsum("ik,cil->ckl", basis_imag, prod_real, precision=highest)
    projection = jnp.concatenate(
        [proj_real.reshape(chan_owned, -1), proj_imag.reshape(chan_owned, -1)], axis=1
    )
    low_real = basis_real.astype(jnp.bfloat16)
    low_imag = basis_imag.astype(jnp.bfloat16)
    sub_real = jnp.einsum("ik,itc->kct", low_real, full_real, preferred_element_type=jnp.float32)
    sub_real = sub_real + jnp.einsum(
        "ik,itc->kct", low_imag, full_imag, preferred_element_type=jnp.float32
    )
    sub_imag = jnp.einsum("ik,itc->kct", low_real, full_imag, preferred_element_type=jnp.float32)
    sub_imag = sub_imag - jnp.einsum(
        "ik,itc->kct", low_imag, full_real, preferred_element_type=jnp.float32
    )
    owned_power = jnp.sum(sub_real * sub_real + sub_imag * sub_imag, axis=0)
    subspace_power = lax.all_to_all(owned_power, "tm", split_axis=1, concat_axis=0, tiled=True)
    return (covariance, projection, subspace_power)


LANES = 128
SUB = 8
ROWS = 16
NT_DIMS = (((1,), (1,)), ((), ()))


def nt_dot(a, b, precision=None):
    return lax.dot_general(a, b, NT_DIMS, precision=precision, preferred_element_type=jnp.float32)


class Plan:
    def __init__(self, voltages, filter_taps):
        self.blocks = lax.axis_size("tm")
        self.devices = lax.axis_size("stn") * self.blocks
        self.taps, self.nfft = filter_taps.shape
        self.chans = self.nfft // 2 // self.devices
        self.inputs = voltages.shape[0] // self.blocks
        self.inputs_all = voltages.shape[0] * lax.axis_size("stn")
        self.frames = voltages.shape[2] // self.nfft
        self.spectra = self.frames * self.blocks
        self.tiles = 2 * self.nfft // LANES
        self.group = LANES // self.spectra
        self.quads = self.chans // max(self.group, 1)

    def packed(self):
        return (
            self.blocks == 2
            and self.group == 4
            and self.group * self.spectra == LANES
            and 2 * self.quads == SUB
            and self.inputs == ROWS
            and self.tiles == ROWS
        )


def table_kernel(plan, rows, taps_ref, out_ref, lanes_ref):
    shape = (rows, LANES)
    row = lax.broadcasted_iota(jnp.int32, shape, 0) + pl.program_id(0) * rows
    lane = lax.broadcasted_iota(jnp.int32, shape, 1)
    per_dest = plan.group * 2 * plan.quads
    dest = lax.div(row, per_dest)
    member = lax.rem(lax.div(row, 2 * plan.quads), plan.group)
    part = lax.rem(lax.div(row, plan.quads), 2)
    quad = lax.rem(row, plan.quads)
    channel = dest * plan.chans + quad * plan.group + member
    unit = 2.0 * math.pi / plan.nfft
    phase = lax.rem(lane * channel + part * (plan.nfft // 4), plan.nfft)
    angle = phase.astype(jnp.float32) * unit
    factor = 1.0 / math.sqrt(plan.nfft)
    cosine = jnp.cos(angle) * factor
    sine = jnp.sin(angle) * factor
    turn = lax.rem(channel * LANES, plan.nfft).astype(jnp.float32) * unit
    turn_cos = jnp.cos(turn)
    turn_sin = jnp.sin(turn)
    spot = lax.div(lax.broadcasted_iota(jnp.int32, (SUB, LANES), 0), 2)

    @pl.when(pl.program_id(0) == 0)
    def _():
        for k in range(plan.taps):
            for sub in range(ROWS // SUB):
                made = jnp.zeros((SUB, LANES), jnp.float32)
                for n in range(SUB // 2):
                    first = (sub * SUB // 2 + n) * LANES
                    line = taps_ref[k : k + 1, first : first + LANES] * (1.0 / 64.0)
                    made = jnp.where(spot == n, jnp.broadcast_to(line, (SUB, LANES)), made)
                at = k * ROWS + sub * SUB
                lanes_ref[at : at + SUB, :] = made

    for tile in range(plan.nfft // LANES):
        first = 2 * tile * LANES
        out_ref[:, first : first + LANES] = cosine.astype(jnp.bfloat16)
        out_ref[:, first + LANES : first + 2 * LANES] = sine.astype(jnp.bfloat16)
        cosine, sine = (
            cosine * turn_cos - sine * turn_sin,
            sine * turn_cos + cosine * turn_sin,
        )


def transform_table(plan, filter_taps):
    rows = 128
    total = plan.nfft
    return pl.pallas_call(
        functools.partial(table_kernel, plan, rows),
        grid=(total // rows,),
        in_specs=[pl.BlockSpec(filter_taps.shape, lambda r: (0, 0))],
        out_specs=[
            pl.BlockSpec((rows, 2 * plan.nfft), lambda r: (r, 0)),
            pl.BlockSpec((plan.taps * ROWS, LANES), lambda r: (0, 0)),
        ],
        out_shape=[
            jax.ShapeDtypeStruct((total, 2 * plan.nfft), jnp.bfloat16),
            jax.ShapeDtypeStruct((plan.taps * ROWS, LANES), jnp.float32),
        ],
        name="table",
    )(filter_taps)


def lane_iota(rows):
    return lax.broadcasted_iota(jnp.int32, (rows, LANES), 1)


def regroup(values):
    lane = lane_iota(SUB)
    low = lane < 64
    even = (lane & 32) == 0
    v0, v1, v2, v3 = values
    x0 = jnp.where(low, v0, pltpu.roll(v2, 64, 1))
    y0 = jnp.where(low, pltpu.roll(v0, 64, 1), v2)
    x1 = jnp.where(low, v1, pltpu.roll(v3, 64, 1))
    y1 = jnp.where(low, pltpu.roll(v1, 64, 1), v3)
    out = []
    for a, b in ((x0, x1), (y0, y1)):
        out.append(jnp.where(even, a, pltpu.roll(b, 32, 1)))
        out.append(jnp.where(even, pltpu.roll(a, 96, 1), b))
    return out


def channelize_kernel(plan, part, where_ref, own_hbm, recv_ref, taps_ref, table_hbm, *refs):
    first_ref = refs[0] if part else None
    outs = refs[1:2] if part else refs[0:2]
    table, own, sig, filt, low, prod, ref_f32, sems = refs[2:]
    half, frames, spectra, taps = plan.inputs // 2, plan.frames, plan.spectra, plan.taps
    span = frames * ROWS
    block = lax.axis_index("tm")
    pieces = 4
    each = half // pieces
    start = pl.multiple_of((block * 2 + part) * (half * span), half * span)
    loads = []
    for n in range(pieces):
        rows = each * span
        source = own_hbm.at[pl.ds(start + n * rows, rows), :]
        loads.append(pltpu.make_async_copy(source, own.at[pl.ds(n * rows, rows), :], sems.at[n]))
    loads.append(pltpu.make_async_copy(table_hbm, table, sems.at[pieces]))
    for load in loads:
        load.start()

    def one_input(i, carry):
        own_at = pl.multiple_of(block * span, span)
        recv_at = pl.multiple_of((1 - block) * span, span)
        at = pl.multiple_of(i * span, span)
        sig[pl.ds(own_at, span), :] = own[pl.ds(at, span), :].astype(jnp.float32)
        sig[pl.ds(recv_at, span), :] = recv_ref[pl.ds(at, span), :].astype(jnp.float32)
        base = pl.multiple_of(i * (spectra * ROWS), spectra * ROWS)
        for sub in range(ROWS // SUB):
            tap = [taps_ref[k * ROWS + sub * SUB : k * ROWS + (sub + 1) * SUB, :] for k in range(taps)]
            data = [sig[f * ROWS + sub * SUB : f * ROWS + (sub + 1) * SUB, :] for f in range(spectra)]
            for t in range(spectra):
                acc = None
                for k in range(max(0, taps - 1 - t), taps):
                    term = tap[k] * data[t - (taps - 1) + k]
                    acc = term if acc is None else acc + term
                filt[pl.ds(base + t * ROWS + sub * SUB, SUB), :] = acc
        return carry

    for n in range(pieces):
        loads[n].wait()
        lax.fori_loop(n * each, (n + 1) * each, one_input, 0)
    for tile in range(plan.tiles):
        picked = filt[pl.ds(tile, half * spectra, stride=ROWS), :]
        low[:, tile * LANES : (tile + 1) * LANES] = picked.astype(jnp.bfloat16)
    loads[pieces].wait()
    prod[...] = nt_dot(table[...], low[...])
    per_dest = plan.group * SUB

    def regrouped(d, cols):
        rows = pl.multiple_of(d * per_dest, per_dest)
        lanes = slice(cols * LANES, (cols + 1) * LANES)
        return regroup([prod[pl.ds(rows + c * SUB, SUB), lanes] for c in range(plan.group)])

    out_ref = outs[0]

    def one_dest(d, carry):
        for cols in range(half // plan.group):
            moved = regrouped(d, cols)
            for b in range(0, plan.group, 2):
                at = (cols * plan.group + b) * SUB
                pair = jnp.concatenate(moved[b : b + 2], axis=0)
                out_ref[d, at : at + 2 * SUB, :] = pair.astype(jnp.bfloat16)
        return carry

    lax.fori_loop(0, plan.devices, one_dest, 0, unroll=8)
    channel = where_ref[0]
    owner = lax.div(channel, plan.chans)
    local = lax.rem(channel, plan.chans)
    quad = lax.div(local, plan.group)
    member = lax.rem(local, plan.group)
    for cols in range(half // plan.group):
        moved = regrouped(owner, cols)
        for b in range(plan.group):
            at = (cols * plan.group + b) * SUB
            ref_f32[at : at + SUB, :] = moved[b]
    lane = lane_iota(SUB)
    shift = LANES - member * spectra
    real = ref_f32[pl.ds(quad, half, stride=SUB), :]
    imag = ref_f32[pl.ds(plan.quads + quad, half, stride=SUB), :]
    real = pltpu.roll(real, lax.rem(shift, LANES), 1)
    imag = pltpu.roll(imag, lax.rem(shift + spectra, LANES), 1)
    both = jnp.where(lane < spectra, real, imag)
    if part == 0:
        outs[1][...] = both
        return
    folded = jnp.where(lane < 2 * spectra, first_ref[...], pltpu.roll(both, 2 * spectra, 1))
    folded = folded.astype(jnp.bfloat16)
    for d in range(plan.devices):
        out_ref[d, half * SUB :, :] = folded


def channelize(plan, part, where, own, recv, taps, table, first):
    half = plan.inputs // 2
    rows = half * plan.frames * ROWS
    whole = pl.BlockSpec(memory_space=pltpu.VMEM)
    hbm = pl.BlockSpec(memory_space=pl.ANY)
    chunk = half * SUB
    out_shape = [jax.ShapeDtypeStruct((plan.devices, chunk + part * SUB, LANES), jnp.bfloat16)]
    if part == 0:
        out_shape.append(jax.ShapeDtypeStruct((half, LANES), jnp.float32))
    return pl.pallas_call(
        functools.partial(channelize_kernel, plan, part),
        in_specs=[pl.BlockSpec(memory_space=pltpu.SMEM), hbm, whole, whole, hbm] + [whole] * part,
        out_specs=[whole] * len(out_shape),
        scratch_shapes=[
            pltpu.VMEM(table.shape, jnp.bfloat16),
            pltpu.VMEM((rows, LANES), jnp.int32),
            pltpu.VMEM((plan.spectra * ROWS, LANES), jnp.float32),
            pltpu.VMEM((half * plan.spectra * ROWS, LANES), jnp.float32),
            pltpu.VMEM((half * plan.spectra, 2 * plan.nfft), jnp.bfloat16),
            pltpu.VMEM((plan.nfft, half * plan.spectra), jnp.float32),
            pltpu.VMEM((half * SUB, LANES), jnp.float32),
            pltpu.SemaphoreType.DMA((5,)),
        ],
        out_shape=out_shape,
    )(where, own, recv, taps, table, *([first] * part))


def inverse_root(value):
    y = lax.rsqrt(value)
    return y * (1.5 - 0.5 * value * y * y)


def basis_kernel(
    plan, count, one_ref, two_ref, picks_ref, x_ref, proj_ref, keep_ref, send_ref, one, two, spot_power, turned_power
):
    highest = lax.Precision.HIGHEST
    span = plan.spectra
    half = plan.inputs // 2
    chunk = half * SUB
    one[...] = one_ref[...].reshape(one.shape).astype(jnp.float32)
    two[...] = two_ref[:, :chunk, :].reshape(two.shape).astype(jnp.float32)
    for n in range(SUB):
        parts = [
            h[pl.ds(n, plan.devices * half, stride=SUB), :].reshape(plan.devices, half, LANES)
            for h in (one, two)
        ]
        x_ref[n] = jnp.concatenate(parts, axis=1).reshape(plan.inputs_all, LANES).astype(jnp.bfloat16)
    folded = two_ref[:, chunk:, :].astype(jnp.float32)
    turned = pltpu.roll(folded.reshape(-1, LANES), 64, 1).reshape(folded.shape)
    ref = jnp.concatenate([folded, turned], axis=1).reshape(plan.inputs_all, LANES)
    ref = ref.astype(jnp.bfloat16)
    rows = lax.broadcasted_iota(jnp.int32, (count, plan.inputs_all), 1)
    onehot = (rows == picks_ref[...]).astype(jnp.float32).astype(jnp.bfloat16)
    chosen = jnp.dot(onehot, ref, preferred_element_type=jnp.float32)
    lane = lane_iota(count)
    zero = jnp.zeros_like(chosen)
    left = jnp.where(lane < 2 * span, chosen, zero)
    cross = jnp.where(
        lane < span,
        -pltpu.roll(chosen, LANES - span, 1),
        jnp.where(lane < 2 * span, pltpu.roll(chosen, span, 1), zero),
    )
    real = nt_dot(left.astype(jnp.bfloat16), ref) / span
    imag = nt_dot(cross.astype(jnp.bfloat16), ref) / span
    index = lax.broadcasted_iota(jnp.int32, real.shape, 0)
    for j in range(count):
        vr = jnp.broadcast_to(real[j : j + 1], real.shape)
        vi = jnp.broadcast_to(imag[j : j + 1], real.shape)
        inner_r = jnp.sum(vr * real + vi * imag, axis=1, keepdims=True)
        inner_i = jnp.sum(vr * imag - vi * real, axis=1, keepdims=True)
        inverse = inverse_root(inner_r[j : j + 1] + 1e-06)
        qr = vr * inverse
        qi = vi * inverse
        inner_r = inner_r * inverse
        inner_i = inner_i * inverse
        later = index > j
        this = index == j
        next_r = real - (qr * inner_r - qi * inner_i)
        next_i = imag - (qr * inner_i + qi * inner_r)
        real = jnp.where(this, qr, jnp.where(later, next_r, real))
        imag = jnp.where(this, qi, jnp.where(later, next_i, imag))
    levels = []
    rest_r, rest_i = real, imag
    for _ in range(3):
        top_r = rest_r.astype(jnp.bfloat16).astype(jnp.float32)
        top_i = rest_i.astype(jnp.bfloat16).astype(jnp.float32)
        levels += [top_r, top_i]
        rest_r = rest_r - top_r
        rest_i = rest_i - top_i
    stack = jnp.concatenate(levels, axis=0).astype(jnp.bfloat16)
    members = plan.group * count
    row = lax.broadcasted_iota(jnp.int32, (members, LANES), 0)
    col = lax.broadcasted_iota(jnp.int32, (members, LANES), 1)
    mine = lax.div(row, count) == lax.div(col, span)
    size = count * count
    lead = lax.broadcasted_iota(jnp.int32, (count, 2 * size), 0)
    spot = lax.broadcasted_iota(jnp.int32, (count, 2 * size), 1)
    fits = lax.rem(spot, count) == lead
    put_r = jnp.where(fits & (spot < size), 1.0, 0.0)
    put_i = jnp.where(fits & (spot >= size), 1.0, 0.0)
    wide = lax.broadcasted_iota(jnp.int32, (members, 2 * size), 1)
    tall = lax.broadcasted_iota(jnp.int32, (members, 2 * size), 0)
    keep = lax.rem(lax.div(wide, count), count) == lax.rem(tall, count)
    own_lanes = lax.broadcasted_iota(jnp.int32, (plan.group, LANES), 0) == lax.div(lane_iota(plan.group), span)
    for quad in range(plan.quads):
        xr = x_ref[quad]
        xi = x_ref[plan.quads + quad]
        sr = jnp.dot(stack, xr, preferred_element_type=jnp.float32)
        si = jnp.dot(stack, xi, preferred_element_type=jnp.float32)
        piece = lambda s, n: s[n * count : (n + 1) * count]
        low_r = piece(sr, 0) + piece(si, 1)
        low_i = piece(si, 0) - piece(sr, 1)
        power = jnp.sum(low_r * low_r + low_i * low_i, axis=0, keepdims=True)
        power = jnp.where(own_lanes, jnp.broadcast_to(power, own_lanes.shape), 0.0)
        spot_power[quad * plan.group : (quad + 1) * plan.group, :] = power
        yr = low_r + ((piece(sr, 2) + piece(si, 3)) + (piece(sr, 4) + piece(si, 5)))
        yi = low_i + ((piece(si, 2) - piece(sr, 3)) + (piece(si, 4) - piece(sr, 5)))
        tiled_r = jnp.where(mine, jnp.concatenate([yr] * plan.group, axis=0), 0.0)
        tiled_i = jnp.where(mine, jnp.concatenate([yi] * plan.group, axis=0), 0.0)
        both = jnp.concatenate([yr, yi], axis=1)
        left_r = jnp.concatenate([tiled_r, tiled_i], axis=1)
        left_i = jnp.concatenate([tiled_i, -tiled_r], axis=1)
        gram_r = nt_dot(left_r, both, highest) / span
        gram_i = nt_dot(left_i, both, highest) / span
        placed = jnp.dot(gram_r, put_r, precision=highest) + jnp.dot(gram_i, put_i, precision=highest)
        placed = jnp.where(keep, placed, 0.0).reshape(plan.group, count, 2 * size)
        proj_ref[quad * plan.group : (quad + 1) * plan.group, :] = jnp.sum(placed, axis=1)
    time = lax.broadcasted_iota(jnp.int32, (span, LANES), 0)
    same = jnp.where(lax.rem(lane_iota(span), span) == time, 1.0, 0.0)
    turned_power[...] = nt_dot(same, spot_power[...], highest)
    block = lax.axis_index("tm")
    keep_ref[...] = turned_power[pl.ds(pl.multiple_of(block * plan.frames, plan.frames), plan.frames), :]
    send_ref[...] = turned_power[pl.ds(pl.multiple_of((1 - block) * plan.frames, plan.frames), plan.frames), :]


def subspace(plan, one, two, basis_inputs):
    count = basis_inputs.shape[0]
    whole = pl.BlockSpec(memory_space=pltpu.VMEM)
    unpacked = pltpu.VMEM((plan.devices * plan.inputs // 2 * SUB, LANES), jnp.float32)
    power = jax.ShapeDtypeStruct((plan.frames, plan.chans), jnp.float32)
    return pl.pallas_call(
        functools.partial(basis_kernel, plan, count),
        in_specs=[whole, whole, whole],
        out_specs=[whole] * 4,
        out_shape=(
            pltpu.VMEM((SUB, plan.inputs_all, LANES), jnp.bfloat16),
            jax.ShapeDtypeStruct((plan.chans, 2 * count * count), jnp.float32),
            power,
            power,
        ),
        scratch_shapes=[
            unpacked,
            unpacked,
            pltpu.VMEM((plan.chans, LANES), jnp.float32),
            pltpu.VMEM((plan.spectra, plan.chans), jnp.float32),
        ],
        name="subspace",
    )(one, two, basis_inputs.reshape(count, 1))


PER_STEP = 2


def covariance_kernel(plan, x_ref, out_ref):
    step = pl.program_id(0)
    quad = lax.div(step * PER_STEP, plan.group)
    real = x_ref[quad]
    imag = x_ref[plan.quads + quad]
    right = jnp.concatenate([real, imag], axis=1)
    total = plan.inputs_all
    for n in range(PER_STEP):
        member = lax.rem(step * PER_STEP, plan.group) + n
        inside = lax.div(lax.broadcasted_iota(jnp.int32, (1, LANES), 1), plan.spectra) == member
        mask = jnp.where(inside, 1.0 / plan.spectra, 0.0).astype(jnp.bfloat16)
        left_r = real * mask
        left_i = imag * mask
        out_ref[n, :, :total] = nt_dot(jnp.concatenate([left_r, left_i], axis=1), right).astype(jnp.bfloat16)
        out_ref[n, :, total:] = nt_dot(jnp.concatenate([left_i, -left_r], axis=1), right).astype(jnp.bfloat16)


def covariances(plan, x):
    out = (plan.chans, plan.inputs_all, 2 * plan.inputs_all)
    return pl.pallas_call(
        functools.partial(covariance_kernel, plan),
        grid=(plan.chans // PER_STEP,),
        in_specs=[pl.BlockSpec(memory_space=pltpu.VMEM)],
        out_specs=pl.BlockSpec((PER_STEP, *out[1:]), lambda c: (c, 0, 0)),
        out_shape=jax.ShapeDtypeStruct(out, jnp.bfloat16),
        name="covariance",
    )(x)


def on_chip(array):
    return pltpu.with_memory_space_constraint(array, pltpu.VMEM)


def packed_plan(plan, voltages, filter_taps, reference_channel, basis_inputs):
    block = lax.axis_index("tm")
    kept = plan.inputs * plan.frames * plan.tiles // 2
    view = voltages.reshape(voltages.shape[0], 2, -1, LANES).transpose(0, 2, 1, 3).reshape(-1, LANES)
    swap = [(0, 1), (1, 0)]
    recv = []
    for part in range(2):
        start = ((1 - block) * 2 + part) * kept
        sent = lax.dynamic_slice_in_dim(view, start, kept, 0).astype(jnp.bfloat16)
        recv.append(lax.ppermute(sent, "tm", swap))
    table, taps = transform_table(plan, filter_taps)
    both = ("stn", "tm")
    recv = [on_chip(r) for r in recv]
    sent, first = channelize(plan, 0, reference_channel, view, recv[0], taps, table, None)
    one = lax.all_to_all(sent, both, split_axis=0, concat_axis=0, tiled=True)
    (sent,) = channelize(plan, 1, reference_channel, view, recv[1], taps, table, first)
    two = lax.all_to_all(sent, both, split_axis=0, concat_axis=0, tiled=True)
    x, projection, keep, send = subspace(plan, on_chip(one), on_chip(two), basis_inputs)
    other = lax.ppermute(send, "tm", swap)
    covariance = covariances(plan, on_chip(x))
    early = jnp.concatenate([keep, other], axis=1)
    late = jnp.concatenate([other, keep], axis=1)
    power = jnp.where(block == 0, early, late)
    return (covariance, projection, power.T)


def on_device(voltages, filter_taps, reference_channel, basis_inputs):
    plan = Plan(voltages, filter_taps)
    if not plan.packed():
        return plain_plan(voltages, filter_taps, reference_channel, basis_inputs)
    return packed_plan(plan, voltages, filter_taps, reference_channel, basis_inputs)


def solution(mesh):
    return jax.shard_map(
        on_device,
        mesh=mesh,
        in_specs=(P("stn", None, "tm"), P(), P(), P()),
        out_specs=(P(("stn", "tm"), None, None), P(("stn", "tm"), None), P("stn", "tm")),
        check_vma=False,
    )
```
